32 devices in a mesh: state: 8 (over y, x, core), snap: 4 (over z).
Axes of the slice: x: 2, y: 2, z: 4, core: 2. Of those that a mesh axis runs over, the one named last changes fastest.
Arguments:
- obs_factor: bfloat16 [8192, 8, 512], P('state', None, 'snap'), may hold values from -1.8920169 to 1.8920169
- ctrl_factor: bfloat16 [8192, 512], P('state', 'snap'), may hold values from -1.6817928 to 1.6817928
- support: int32 [64, 4], P('state'), may hold values from 0 to 1
Outputs:
- cross: float32 [8, 512, 512], P(None, 'snap', 'state')
The draws below stay inside these ranges and needn't reach their ends.
All inputs are finite; a program needn't handle non-finite values.
Results may differ from the reference program's by a relative error of at most 0.0006.
Values may be sent and summed in bfloat16 or wider, within the bound.
A program may use at most 64 MiB of HBM per device.

```python
import math
import jax
import jax.numpy as jnp
from jax import lax

W = 512
NWIN = 8
ROWS = 8192
RBLOCKS = 64
NCB = 4


def common_rows(key):
    base = jax.random.truncated_normal(jax.random.fold_in(key, 11), -5.0, 5.0, (ROWS, W), jnp.float32)
    row_scale = jnp.ones((ROWS, 1), jnp.float32)
    return (base, row_scale)


def draw_ctrl_factor(key, part):
    base, row_scale = common_rows(key)
    factor = ROWS ** (-0.25) * row_scale * base
    return factor.astype(jnp.bfloat16)


def draw_obs_factor(key, part):
    base, row_scale = common_rows(key)
    other = jax.random.truncated_normal(jax.random.fold_in(key, 13), -5.0, 5.0, (ROWS, NWIN, W), jnp.float32)
    weight = 3.0 * ROWS ** (-0.5)
    factor = ROWS ** (-0.25) * row_scale[:, :, None] * (other + weight * base[:, None, :])
    return factor.astype(jnp.bfloat16)


def draw_support(key, part):
    scores = jax.random.randint(jax.random.fold_in(key, 17), (RBLOCKS, NCB), 0, 100)
    block_index = jnp.arange(RBLOCKS, dtype=jnp.int32)[:, None]
    limits = 20 + 70 * block_index // RBLOCKS
    return (scores < limits).astype(jnp.int32)


def setup_inputs(seed: int = 0) -> dict:
    key_list = jax.random.split(jax.random.key(seed), 4)
    return {
        "obs_factor": draw_obs_factor(jax.random.fold_in(key_list[3], 71), 0),
        "ctrl_factor": draw_ctrl_factor(jax.random.fold_in(key_list[3], 71), 0),
        "support": draw_support(jax.random.fold_in(key_list[3], 71), 0),
    }


def reference(obs_factor, ctrl_factor, support):
    row_blocks = support.shape[0]
    windows = obs_factor.shape[1]
    width = ctrl_factor.shape[1]
    block_rows = obs_factor.shape[0] // row_blocks
    group = math.gcd(row_blocks, 16)
    turn_count = row_blocks // group
    obs_groups = obs_factor.reshape(turn_count, group, block_rows, windows, width)
    ctrl_groups = ctrl_factor.reshape(turn_count, group, block_rows, width)
    sup_groups = support.reshape(turn_count, group, support.shape[1])

    def accumulate(total, items):
        obs_part, ctrl_part, sup_part = items
        keep_mask = jnp.repeat(sup_part, width // sup_part.shape[-1], axis=-1).astype(jnp.float32)
        obs_kept = obs_part.astype(jnp.float32) * keep_mask[:, None, None, :]
        ctrl_kept = ctrl_part.astype(jnp.float32) * keep_mask[:, None, :]
        term = jnp.einsum("grwi,grj->wij", obs_kept, ctrl_kept, precision=lax.Precision.HIGHEST)
        return total + term, None

    start_total = jnp.zeros((windows, width, width), jnp.float32)
    total, _ = lax.scan(accumulate, start_total, (obs_groups, ctrl_groups, sup_groups))
    return total
```

```python
import functools

import jax
import jax.numpy as jnp
from jax import lax
from jax.experimental import pallas as pl
from jax.experimental.pallas import tpu as pltpu
from jax.sharding import PartitionSpec as P

MESH = pl.DeviceIdType.MESH
CORES = 2
SIDE = 2
PLANE = CORES * SIDE * SIDE
LINE = SIDE * SIDE
QS = 4
RELAY_FROM = QS // 2
BEHIND_MIDDLE = 4
BEHIND_END = 2
PAIR = 2
RELAY_AT = {2: 4, 3: 6, 4: 10, 5: 12, 6: 13, 7: 14}
VMEM_BYTES = 54900 * 1024


def cross_kernel(
    support_hbm,
    obs_hbm,
    ctrl_hbm,
    out,
    support,
    obs_raw,
    ctrl_raw,
    wide,
    obs,
    own_t,
    ctrl_t,
    part,
    far,
    near,
    ld_sem,
    obs_send,
    obs_recv,
    own_send,
    pair_send,
    fwd_send,
    ctrl_recv,
    half_send,
    half_recv,
    far_send,
    far_recv,
):
    s = lax.axis_index("state")
    z = lax.axis_index("snap")
    row_blocks = support_hbm.shape[1]
    rows, windows, cols = obs_hbm.shape
    block = rows // row_blocks
    piece = ctrl_t.shape[3]
    h = s % CORES
    chip = s // CORES
    ax = chip % SIDE
    ay = chip // SIDE
    pair = chip * CORES + (1 - h)
    x_next = (ay * SIDE + (1 - ax)) * CORES + h
    y_next = ((1 - ay) * SIDE + ax) * CORES + h
    last = LINE - 1
    middle = jnp.logical_and(z > 0, z < last)

    def load_ctrl():
        return pltpu.make_async_copy(ctrl_hbm, ctrl_raw, ld_sem.at[row_blocks])

    def load_obs(k):
        span = pl.ds(k * block, block)
        return pltpu.make_async_copy(obs_hbm.at[span], obs_raw.at[span], ld_sem.at[k])

    def load_support():
        return pltpu.make_async_copy(support_hbm, support, ld_sem.at[row_blocks + 1])

    load_ctrl().start()
    load_support().start()
    barrier = pltpu.get_barrier_semaphore()

    def greet(state, snap):
        pl.semaphore_signal(barrier, inc=1, device_id=(state, snap), device_id_type=MESH)

    greet(pair, z)
    greet(x_next, z)
    greet(y_next, z)

    @pl.when(z > 0)
    def _():
        greet(s, z - 1)
        greet(pair, z - 1)

    @pl.when(z < last)
    def _():
        greet(s, z + 1)
        greet(pair, z + 1)

    for k in range(row_blocks):
        load_obs(k).start()

    load_support().wait()
    load_ctrl().wait()
    for k in range(row_blocks):
        span = slice(k * block, (k + 1) * block)
        keep = support[z, k].astype(jnp.float32)
        kept = ctrl_raw[span, :] * keep.astype(jnp.bfloat16)
        turned = kept.T
        own_t[:, :, span] = turned.reshape(CORES * QS, piece, block)

    @pl.when(middle)
    def _():
        pl.semaphore_wait(barrier, 7)

    @pl.when(jnp.logical_not(middle))
    def _():
        pl.semaphore_wait(barrier, 5)

    def own_copy(side, q, g):
        state = chip * CORES + g
        snap = z + 2 * side - 1
        return pltpu.make_async_remote_copy(
            src_ref=own_t.at[g * QS + q],
            dst_ref=ctrl_t.at[z, q, h],
            send_sem=own_send.at[side, q, g],
            recv_sem=ctrl_recv.at[z, q, h],
            device_id=(state, snap),
            device_id_type=MESH,
        )

    def pair_copy(q):
        return pltpu.make_async_remote_copy(
            src_ref=own_t.at[(1 - h) * QS + q],
            dst_ref=ctrl_t.at[z, q, h],
            send_sem=pair_send.at[q],
            recv_sem=ctrl_recv.at[z, q, h],
            device_id=(pair, z),
            device_id_type=MESH,
        )

    def fwd_copy(b, q, hs, snap):
        return pltpu.make_async_remote_copy(
            src_ref=ctrl_t.at[b, q, hs],
            dst_ref=ctrl_t.at[b, q, hs],
            send_sem=fwd_send.at[b, q, hs],
            recv_sem=ctrl_recv.at[b, q, hs],
            device_id=(s, snap),
            device_id_type=MESH,
        )

    def arrived(b, q, hs):
        fwd_copy(b, q, hs, z).wait_recv()

    for q in range(QS):
        for g in range(CORES):

            @pl.when(z > 0)
            def _():
                own_copy(0, q, g).start()

            @pl.when(z < last)
            def _():
                own_copy(1, q, g).start()

    for q in range(QS):
        pair_copy(q).start()
        ctrl_t[z, q, h] = own_t[h * QS + q]

    def obs_copy(k):
        span = pl.ds(pl.multiple_of(k * block, block), block)
        return pltpu.make_async_remote_copy(
            src_ref=obs.at[h, span],
            dst_ref=obs.at[h, span],
            send_sem=obs_send.at[k],
            recv_sem=obs_recv.at[k],
            device_id=(pair, z),
            device_id_type=MESH,
        )

    def arrange(k, _):
        load_obs(k).wait()
        span = pl.ds(pl.multiple_of(k * block, block), block)
        keep = support[z, k].astype(jnp.float32)
        raw = obs_raw[span].astype(jnp.float32) * keep
        wide[...] = raw.reshape(block * windows, cols)
        for w in range(windows):
            obs[h, span, w * cols : (w + 1) * cols] = wide[
                pl.ds(w, block, stride=windows), :
            ].astype(jnp.bfloat16)
        obs_copy(k).start()
        return 0

    lax.fori_loop(0, row_blocks, arrange, 0)

    def pass_on(d, q):
        @pl.when(jnp.logical_and(middle, z - d >= 0))
        def _():
            for hs in range(CORES):
                arrived(z - d, q, hs)
                fwd_copy(z - d, q, hs, z + 1).start()

        @pl.when(jnp.logical_and(middle, z + d <= last))
        def _():
            for hs in range(CORES):
                arrived(z + d, q, hs)
                fwd_copy(z + d, q, hs, z - 1).start()

    def block_at(k):
        up = jnp.where(k == 0, 0, jnp.where(k == 1, 1, jnp.where(k == 2, 2, 3)))
        one = jnp.where(k == 0, 1, jnp.where(k == 1, 2, jnp.where(k == 2, 0, 3)))
        return jnp.where(
            z == 0, up, jnp.where(z == last, last - up, jnp.where(z == 1, one, last - one))
        )

    def half_copy(kind, q, rows_half, b, state):
        return pltpu.make_async_remote_copy(
            src_ref=part.at[b, q, rows_half],
            dst_ref=far.at[kind, q],
            send_sem=half_send.at[kind, q],
            recv_sem=half_recv.at[kind, q],
            device_id=(state, z),
            device_id_type=MESH,
        )

    def near_copy(kind, q, rows_half, b, state):
        return pltpu.make_async_remote_copy(
            src_ref=part.at[b, q, rows_half],
            dst_ref=near.at[kind, q, rows_half],
            send_sem=far_send.at[kind, q, rows_half],
            recv_sem=far_recv.at[kind, q, rows_half],
            device_id=(state, z),
            device_id_type=MESH,
        )

    def role(b):
        same_x = b % SIDE == ax
        same_y = b // SIDE == ay
        kind = jnp.where(same_x, 1, 0)
        beside = same_x != same_y
        corner = jnp.logical_and(jnp.logical_not(same_x), jnp.logical_not(same_y))
        return kind, beside, corner

    def finished(t):
        behind = jnp.where(middle, BEHIND_MIDDLE, BEHIND_END)
        return jnp.maximum(jnp.minimum(2 * t - 3 * QS, t - behind + 1), 0)

    def finish(t, _):
        b = block_at(t // QS)
        q = t % QS
        kind, beside, _ = role(b)

        @pl.when(beside)
        def _():
            half_copy(kind, q, kind, b, y_next).wait_recv()
            part[b, q, kind] = part[b, q, kind] + far[kind, q]
            near_copy(kind, q, kind, b, jnp.where(kind == 1, y_next, x_next)).start()

        return 0

    tile = 2 * cols
    width = obs.shape[2]

    def turn(t, before, after, count):
        b = block_at(t // QS)
        q = t % QS

        if count == QS:
            for i in range(count):
                arrived(b, q + i, 1 - h)
        else:
            for k, when in RELAY_AT.items():

                @pl.when(t == when)
                def _():
                    pass_on(1 + k // QS, k % QS)

        if count == 1:

            @pl.when(jnp.logical_not(middle))
            def _():
                for hs in range(CORES):
                    arrived(b, q, hs)

        left = [
            ctrl_t[b, pl.ds(q, count), hs].reshape(count * piece, obs.shape[1])
            for hs in range(CORES)
        ]
        for n in range(0, width, tile):
            total = sum(
                jnp.dot(
                    left[hs], obs[hs, :, n : n + tile], preferred_element_type=jnp.float32
                )
                for hs in range(CORES)
            )
            part[b, pl.ds(q, count), :, :, n : n + tile] = total.reshape(
                count, 2, piece // 2, tile
            )

        kind, beside, corner = role(b)

        @pl.when(beside)
        def _():
            for i in range(count):
                state = jnp.where(kind == 1, y_next, x_next)
                near_copy(kind, q + i, 1 - kind, b, state).start()

        @pl.when(corner)
        def _():
            for i in range(count):
                half_copy(0, q + i, 0, b, y_next).start()
                half_copy(1, q + i, 1, b, x_next).start()

        if count < QS:
            lax.fori_loop(before, after, finish, 0)
        return 0

    singles = jnp.where(middle, (LINE - 1) * QS, QS)

    def double(i, _):
        t = QS + i * PAIR
        return turn(t, finished(t - 1), finished(t + PAIR - 1), PAIR)

    def single(t, _):
        return turn(t, finished(t - 1), finished(t), 1)

    for k in range(RELAY_FROM):
        pass_on(1, k)
    for k in range(row_blocks):
        obs_copy(k).wait_recv()
    turn(0, 0, 0, QS)
    lax.fori_loop(0, (singles - QS) // PAIR, double, 0)
    lax.fori_loop(singles, LINE * QS, single, 0)
    lax.fori_loop(finished(LINE * QS - 1), LINE * QS, finish, 0)

    for q in range(QS):
        for r in range(2):
            for kind in range(2):
                near_copy(kind, q, r, chip, s).wait_recv()
            total = part[chip, q, r] + near[0, q, r] + near[1, q, r]
            base = (q * 2 + r) * (piece // 2)
            for w in range(windows):
                out[w, base : base + piece // 2, :] = total[:, w * cols : (w + 1) * cols]

    for q in range(QS):
        for kind in range(2):
            half_copy(kind, q, kind, chip, y_next).wait_send()
            for r in range(2):
                near_copy(kind, q, r, chip, y_next).wait_send()
        pair_copy(q).wait_send()
        for g in range(CORES):

            @pl.when(z > 0)
            def _():
                own_copy(0, q, g).wait_send()

            @pl.when(z < last)
            def _():
                own_copy(1, q, g).wait_send()

        for d in range(1, LINE - 1):
            for hs in range(CORES):

                @pl.when(jnp.logical_and(middle, z - d >= 0))
                def _():
                    fwd_copy(z - d, q, hs, z).wait_send()

                @pl.when(jnp.logical_and(middle, z + d <= last))
                def _():
                    fwd_copy(z + d, q, hs, z).wait_send()

    for k in range(row_blocks):
        obs_copy(k).wait_send()


def plane_local(obs_factor, ctrl_factor, support):
    rows, windows, cols = obs_factor.shape
    row_blocks = support.shape[0]
    piece = cols // (CORES * QS)
    width = windows * cols
    bf16, f32 = jnp.bfloat16, jnp.float32
    dma = pltpu.SemaphoreType.DMA
    turned = pl.pallas_call(
        cross_kernel,
        out_shape=jax.ShapeDtypeStruct((windows, cols // CORES, cols), f32),
        in_specs=[
            pl.BlockSpec(memory_space=pltpu.HBM),
            pl.BlockSpec(memory_space=pltpu.HBM),
            pl.BlockSpec(memory_space=pltpu.HBM),
        ],
        out_specs=pl.BlockSpec(memory_space=pltpu.VMEM),
        scratch_shapes=[
            pltpu.SMEM((support.shape[1], row_blocks), jnp.int32),
            pltpu.VMEM((rows, windows, cols), bf16),
            pltpu.VMEM((rows, cols), bf16),
            pltpu.VMEM((rows // row_blocks * windows, cols), f32),
            pltpu.VMEM((CORES, rows, width), bf16),
            pltpu.VMEM((CORES * QS, piece, rows), bf16),
            pltpu.VMEM((LINE, QS, CORES, piece, rows), bf16),
            pltpu.VMEM((LINE, QS, 2, piece // 2, width), f32),
            pltpu.VMEM((2, QS, piece // 2, width), f32),
            pltpu.VMEM((2, QS, 2, piece // 2, width), f32),
            dma((row_blocks + 2,)),
            dma((row_blocks,)),
            dma((row_blocks,)),
            dma((2, QS, CORES)),
            dma((QS,)),
            dma((LINE, QS, CORES)),
            dma((LINE, QS, CORES)),
            dma((2, QS)),
            dma((2, QS)),
            dma((2, QS, 2)),
            dma((2, QS, 2)),
        ],
        compiler_params=pltpu.CompilerParams(
            collective_id=0, has_side_effects=True, vmem_limit_bytes=VMEM_BYTES
        ),
        name="masked_cross",
    )(support.T, obs_factor, ctrl_factor)
    return jnp.swapaxes(turned, 1, 2)


def mask_local(obs_factor, ctrl_factor, support):
    local_cols = ctrl_factor.shape[1]
    total_cols = lax.axis_size("snap") * local_cols
    col_block = total_cols // support.shape[1]
    blocks_here = local_cols // col_block
    first_block = lax.axis_index("snap") * blocks_here
    owned_blocks = lax.dynamic_slice_in_dim(support, first_block, blocks_here, 1)
    keep_mask = jnp.repeat(owned_blocks, col_block, axis=1).astype(jnp.bfloat16)
    row_blocks = support.shape[0]
    total_rows, windows, _ = obs_factor.shape
    obs_kept = (
        obs_factor.reshape(row_blocks, total_rows // row_blocks, windows, local_cols)
        * keep_mask[:, None, None, :]
    )
    ctrl_kept = (
        ctrl_factor.reshape(row_blocks, total_rows // row_blocks, local_cols)
        * keep_mask[:, None, :]
    )
    return (obs_kept.reshape(obs_factor.shape), ctrl_kept.reshape(ctrl_factor.shape))


def general_local(obs_factor, ctrl_factor, support):
    obs_kept, ctrl_kept = mask_local(obs_factor, ctrl_factor, support)
    band_rows = jnp.einsum(
        "rwi,rj->wij",
        obs_kept,
        lax.all_gather(ctrl_kept, "snap", axis=1, tiled=True),
        preferred_element_type=jnp.float32,
    )
    return lax.psum_scatter(band_rows, "state", scatter_dimension=2, tiled=True)


def solution(mesh):
    in_specs = (P("state", None, "snap"), P("state", "snap"), P("state", None))
    out_specs = P(None, "snap", "state")
    fits = mesh.shape["state"] == PLANE and mesh.shape["snap"] == LINE
    body = plane_local if fits else general_local
    return jax.shard_map(body, mesh=mesh, in_specs=in_specs, out_specs=out_specs, check_vma=False)
```

```python
import functools

import jax
import jax.numpy as jnp
from jax import lax
from jax.experimental import pallas as pl
from jax.experimental.pallas import tpu as pltpu
from jax.sharding import PartitionSpec as P

MESH = pl.DeviceIdType.MESH
CORES = 2
SIDE = 2
PLANE = CORES * SIDE * SIDE
LINE = SIDE * SIDE
QS = 4
LAG_MIDDLE = 3
RAMP_MIDDLE = 12
LAG_END = 1
RAMP_END = 12
PAIR = 2
RELAY_AT = ((1, 2, 4), (1, 3, 6), (2, 0, 10), (2, 1, 12), (2, 2, 13), (2, 3, 14))
EARLY = QS // 2
SINGLES_MIDDLE = (LINE - 1) * QS
VMEM_BYTES = 54900 * 1024


def cross_kernel(
    support_hbm,
    obs_hbm,
    ctrl_hbm,
    out,
    support,
    obs_raw,
    ctrl_raw,
    wide,
    obs,
    own_t,
    ctrl_t,
    part,
    far,
    near,
    ld_sem,
    obs_send,
    obs_recv,
    own_send,
    pair_send,
    fwd_send,
    ctrl_recv,
    half_send,
    half_recv,
    far_send,
    far_recv,
):
    s = lax.axis_index("state")
    z = lax.axis_index("snap")
    row_blocks = support_hbm.shape[1]
    rows, windows, cols = obs_hbm.shape
    block = rows // row_blocks
    piece = ctrl_t.shape[3]
    h = s % CORES
    chip = s // CORES
    ax = chip % SIDE
    ay = chip // SIDE
    pair = chip * CORES + (1 - h)
    x_next = (ay * SIDE + (1 - ax)) * CORES + h
    y_next = ((1 - ay) * SIDE + ax) * CORES + h
    last = LINE - 1
    middle = jnp.logical_and(z > 0, z < last)

    def load_ctrl():
        return pltpu.make_async_copy(ctrl_hbm, ctrl_raw, ld_sem.at[row_blocks])

    def load_obs(k):
        span = pl.ds(k * block, block)
        return pltpu.make_async_copy(obs_hbm.at[span], obs_raw.at[span], ld_sem.at[k])

    def load_support():
        return pltpu.make_async_copy(support_hbm, support, ld_sem.at[row_blocks + 1])

    load_ctrl().start()
    load_support().start()
    barrier = pltpu.get_barrier_semaphore()

    def greet(state, snap):
        pl.semaphore_signal(barrier, inc=1, device_id=(state, snap), device_id_type=MESH)

    greet(pair, z)
    greet(x_next, z)
    greet(y_next, z)

    @pl.when(z > 0)
    def _():
        greet(s, z - 1)
        greet(pair, z - 1)

    @pl.when(z < last)
    def _():
        greet(s, z + 1)
        greet(pair, z + 1)

    for k in range(row_blocks):
        load_obs(k).start()

    load_support().wait()
    load_ctrl().wait()
    for k in range(row_blocks):
        span = slice(k * block, (k + 1) * block)
        keep = support[z, k].astype(jnp.float32)
        kept = ctrl_raw[span, :] * keep.astype(jnp.bfloat16)
        turned = kept.T
        own_t[:, :, span] = turned.reshape(CORES * QS, piece, block)

    @pl.when(middle)
    def _():
        pl.semaphore_wait(barrier, 7)

    @pl.when(jnp.logical_not(middle))
    def _():
        pl.semaphore_wait(barrier, 5)

    def own_copy(side, q, g):
        state = chip * CORES + g
        snap = z + 2 * side - 1
        return pltpu.make_async_remote_copy(
            src_ref=own_t.at[g * QS + q],
            dst_ref=ctrl_t.at[z, q, h],
            send_sem=own_send.at[side],
            recv_sem=ctrl_recv.at[z, q],
            device_id=(state, snap),
            device_id_type=MESH,
        )

    def pair_copy(q):
        return pltpu.make_async_remote_copy(
            src_ref=own_t.at[(1 - h) * QS + q],
            dst_ref=ctrl_t.at[z, q, h],
            send_sem=pair_send,
            recv_sem=ctrl_recv.at[z, q],
            device_id=(pair, z),
            device_id_type=MESH,
        )

    def fwd_copy(b, q, hs, snap):
        return pltpu.make_async_remote_copy(
            src_ref=ctrl_t.at[b, q, hs],
            dst_ref=ctrl_t.at[b, q, hs],
            send_sem=fwd_send.at[b],
            recv_sem=ctrl_recv.at[b, q],
            device_id=(s, snap),
            device_id_type=MESH,
        )

    def span_of(ref, send, recv):
        return pltpu.make_async_remote_copy(
            src_ref=ref,
            dst_ref=ref,
            send_sem=send,
            recv_sem=recv,
            device_id=(pair, z),
            device_id_type=MESH,
        )

    def arrived(b, q):
        span_of(ctrl_t.at[b, q], pair_send, ctrl_recv.at[b, q]).wait_recv()

    def own_out(q):
        for g in range(CORES):

            @pl.when(z > 0)
            def _():
                own_copy(0, q, g).start()

            @pl.when(z < last)
            def _():
                own_copy(1, q, g).start()

    for q in range(QS):
        own_out(q)

    for q in range(QS):
        pair_copy(q).start()
        ctrl_t[z, q, h] = own_t[h * QS + q]

    def obs_copy(k):
        span = pl.ds(pl.multiple_of(k * block, block), block)
        return pltpu.make_async_remote_copy(
            src_ref=obs.at[h, span],
            dst_ref=obs.at[h, span],
            send_sem=obs_send,
            recv_sem=obs_recv,
            device_id=(pair, z),
            device_id_type=MESH,
        )

    def arrange(k, _):
        load_obs(k).wait()
        span = pl.ds(pl.multiple_of(k * block, block), block)
        keep = support[z, k].astype(jnp.float32)
        raw = obs_raw[span].astype(jnp.float32) * keep
        wide[...] = raw.reshape(block * windows, cols)
        for w in range(windows):
            obs[h, span, w * cols : (w + 1) * cols] = wide[
                pl.ds(w, block, stride=windows), :
            ].astype(jnp.bfloat16)
        obs_copy(k).start()
        return 0

    lax.fori_loop(0, row_blocks, arrange, 0)

    def pass_on(d, q):
        @pl.when(jnp.logical_and(middle, z - d >= 0))
        def _():
            arrived(z - d, q)
            for hs in range(CORES):
                fwd_copy(z - d, q, hs, z + 1).start()

        @pl.when(jnp.logical_and(middle, z + d <= last))
        def _():
            arrived(z + d, q)
            for hs in range(CORES):
                fwd_copy(z + d, q, hs, z - 1).start()

    def block_at(k):
        up = jnp.where(k == 0, 0, jnp.where(k == 1, 1, jnp.where(k == 2, 2, 3)))
        one = jnp.where(k == 0, 1, jnp.where(k == 1, 2, jnp.where(k == 2, 0, 3)))
        return jnp.where(
            z == 0, up, jnp.where(z == last, last - up, jnp.where(z == 1, one, last - one))
        )

    def piece_at(t):
        return block_at(t // QS), t % QS

    def half_copy(kind, q, rows_half, b, state):
        return pltpu.make_async_remote_copy(
            src_ref=part.at[b, q, rows_half],
            dst_ref=far.at[kind, q],
            send_sem=half_send,
            recv_sem=half_recv.at[kind, q],
            device_id=(state, z),
            device_id_type=MESH,
        )

    def near_copy(kind, q, rows_half, b, state):
        return pltpu.make_async_remote_copy(
            src_ref=part.at[b, q, rows_half],
            dst_ref=near.at[q, kind, rows_half],
            send_sem=far_send,
            recv_sem=far_recv.at[q],
            device_id=(state, z),
            device_id_type=MESH,
        )

    def role(b):
        same_x = b % SIDE == ax
        same_y = b // SIDE == ay
        kind = jnp.where(same_x, 1, 0)
        beside = same_x != same_y
        corner = jnp.logical_and(jnp.logical_not(same_x), jnp.logical_not(same_y))
        return kind, beside, corner

    def finished(t):
        lag = jnp.where(middle, LAG_MIDDLE, LAG_END)
        ramp = jnp.where(middle, RAMP_MIDDLE, RAMP_END)
        return jnp.maximum(jnp.minimum(2 * t - ramp, t - lag), 0)

    def finish(t, _):
        b, q = piece_at(t)
        kind, beside, _ = role(b)

        @pl.when(beside)
        def _():
            half_copy(kind, q, kind, b, y_next).wait_recv()
            part[b, q, kind] = part[b, q, kind] + far[kind, q]
            near_copy(kind, q, kind, b, jnp.where(kind == 1, y_next, x_next)).start()

        return 0

    tile = 2 * cols
    width = obs.shape[2]

    def turn(t, before, after, count):
        b, q = piece_at(t)

        if count == QS:
            for i in range(count):
                span_of(
                    ctrl_t.at[b, i, 1 - h], pair_send, ctrl_recv.at[b, i]
                ).wait_recv()

        if count < QS:
            for d, k, when in RELAY_AT:

                @pl.when(t == when)
                def _():
                    pass_on(d, k)

        if count == 1:

            @pl.when(jnp.logical_not(middle))
            def _():
                arrived(b, q)

        left = [
            ctrl_t[b, pl.ds(q, count), hs].reshape(count * piece, obs.shape[1])
            for hs in range(CORES)
        ]
        for n in range(0, width, tile):
            total = sum(
                jnp.dot(
                    left[hs], obs[hs, :, n : n + tile], preferred_element_type=jnp.float32
                )
                for hs in range(CORES)
            )
            part[b, pl.ds(q, count), :, :, n : n + tile] = total.reshape(
                count, 2, piece // 2, tile
            )

        kind, beside, corner = role(b)

        @pl.when(beside)
        def _():
            for i in range(count):
                state = jnp.where(kind == 1, y_next, x_next)
                near_copy(kind, q + i, 1 - kind, b, state).start()

        @pl.when(corner)
        def _():
            for i in range(count):
                half_copy(0, q + i, 0, b, y_next).start()
                half_copy(1, q + i, 1, b, x_next).start()

        if count < QS:
            lax.fori_loop(before, after, finish, 0)
        return 0

    singles = jnp.where(middle, SINGLES_MIDDLE, QS)

    def double(i, _):
        t = QS + i * PAIR
        return turn(t, finished(t - 1), finished(t + PAIR - 1), PAIR)

    def single(t, _):
        return turn(t, finished(t - 1), finished(t), 1)

    for k in range(EARLY):
        pass_on(1, k)

    span_of(obs.at[1 - h], obs_send, obs_recv).wait_recv()
    turn(0, 0, 0, QS)
    lax.fori_loop(0, (singles - QS) // PAIR, double, 0)
    lax.fori_loop(singles, LINE * QS, single, 0)
    lax.fori_loop(finished(LINE * QS - 1), LINE * QS, finish, 0)

    for q in range(QS):
        span_of(near.at[q], far_send, far_recv.at[q]).wait_recv()
        for r in range(2):
            total = part[chip, q, r] + near[q, 0, r] + near[q, 1, r]
            base = (q * 2 + r) * (piece // 2)
            for w in range(windows):
                out[w, base : base + piece // 2, :] = total[:, w * cols : (w + 1) * cols]

    span_of(part.at[0], half_send, half_send).wait_send()
    span_of(near, far_send, far_send).wait_send()
    span_of(own_t.at[pl.ds(0, QS)], pair_send, pair_send).wait_send()
    span_of(obs.at[h], obs_send, obs_send).wait_send()

    @pl.when(z > 0)
    def _():
        span_of(own_t, own_send.at[0], own_send.at[0]).wait_send()

    @pl.when(z < last)
    def _():
        span_of(own_t, own_send.at[1], own_send.at[1]).wait_send()

    for d in range(1, LINE - 1):

        @pl.when(jnp.logical_and(middle, z - d >= 0))
        def _():
            span_of(ctrl_t.at[z - d], fwd_send.at[z - d], pair_send).wait_send()

        @pl.when(jnp.logical_and(middle, z + d <= last))
        def _():
            span_of(ctrl_t.at[z + d], fwd_send.at[z + d], pair_send).wait_send()


def plane_local(obs_factor, ctrl_factor, support):
    rows, windows, cols = obs_factor.shape
    row_blocks = support.shape[0]
    piece = cols // (CORES * QS)
    width = windows * cols
    bf16, f32 = jnp.bfloat16, jnp.float32
    dma = pltpu.SemaphoreType.DMA
    turned = pl.pallas_call(
        cross_kernel,
        out_shape=jax.ShapeDtypeStruct((windows, cols // CORES, cols), f32),
        in_specs=[
            pl.BlockSpec(memory_space=pltpu.HBM),
            pl.BlockSpec(memory_space=pltpu.HBM),
            pl.BlockSpec(memory_space=pltpu.HBM),
        ],
        out_specs=pl.BlockSpec(memory_space=pltpu.VMEM),
        scratch_shapes=[
            pltpu.SMEM((support.shape[1], row_blocks), jnp.int32),
            pltpu.VMEM((rows, windows, cols), bf16),
            pltpu.VMEM((rows, cols), bf16),
            pltpu.VMEM((rows // row_blocks * windows, cols), f32),
            pltpu.VMEM((CORES, rows, width), bf16),
            pltpu.VMEM((CORES * QS, piece, rows), bf16),
            pltpu.VMEM((LINE, QS, CORES, piece, rows), bf16),
            pltpu.VMEM((LINE, QS, 2, piece // 2, width), f32),
            pltpu.VMEM((2, QS, piece // 2, width), f32),
            pltpu.VMEM((QS, 2, 2, piece // 2, width), f32),
            dma((row_blocks + 2,)),
            dma,
            dma,
            dma((2,)),
            dma,
            dma((LINE,)),
            dma((LINE, QS)),
            dma,
            dma((2, QS)),
            dma,
            dma((QS,)),
        ],
        compiler_params=pltpu.CompilerParams(
            collective_id=0, has_side_effects=True, vmem_limit_bytes=VMEM_BYTES
        ),
        name="masked_cross",
    )(support.T, obs_factor, ctrl_factor)
    return jnp.swapaxes(turned, 1, 2)


def mask_local(obs_factor, ctrl_factor, support):
    local_cols = ctrl_factor.shape[1]
    total_cols = lax.axis_size("snap") * local_cols
    col_block = total_cols // support.shape[1]
    blocks_here = local_cols // col_block
    first_block = lax.axis_index("snap") * blocks_here
    owned_blocks = lax.dynamic_slice_in_dim(support, first_block, blocks_here, 1)
    keep_mask = jnp.repeat(owned_blocks, col_block, axis=1).astype(jnp.bfloat16)
    row_blocks = support.shape[0]
    total_rows, windows, _ = obs_factor.shape
    obs_kept = (
        obs_factor.reshape(row_blocks, total_rows // row_blocks, windows, local_cols)
        * keep_mask[:, None, None, :]
    )
    ctrl_kept = (
        ctrl_factor.reshape(row_blocks, total_rows // row_blocks, local_cols)
        * keep_mask[:, None, :]
    )
    return (obs_kept.reshape(obs_factor.shape), ctrl_kept.reshape(ctrl_factor.shape))


def general_local(obs_factor, ctrl_factor, support):
    obs_kept, ctrl_kept = mask_local(obs_factor, ctrl_factor, support)
    band_rows = jnp.einsum(
        "rwi,rj->wij",
        obs_kept,
        lax.all_gather(ctrl_kept, "snap", axis=1, tiled=True),
        preferred_element_type=jnp.float32,
    )
    return lax.psum_scatter(band_rows, "state", scatter_dimension=2, tiled=True)


def solution(mesh):
    in_specs = (P("state", None, "snap"), P("state", "snap"), P("state", None))
    out_specs = P(None, "snap", "state")
    fits = mesh.shape["state"] == PLANE and mesh.shape["snap"] == LINE
    body = plane_local if fits else general_local
    return jax.shard_map(body, mesh=mesh, in_specs=in_specs, out_specs=out_specs, check_vma=False)
```
